128 devices in a mesh: gx: 8 (over y, core), gy: 16 (over z, x).
Axes of the slice: x: 4, y: 4, z: 4, core: 2. Of those that a mesh axis runs over, the one named last changes fastest.
Arguments:
- stream: bfloat16 [768, 16384], P('gy', 'gx'), may hold values from -120 to 120
- attn_gain: bfloat16 [16384], P('gx'), may hold values from 0.099609375 to 1.8984375
- ffn_gain: bfloat16 [16384], P('gx'), may hold values from 0.099609375 to 1.8984375
- w_query: bfloat16 [16384, 16384], P('gx', 'gy'), may hold values from -0.046875 to 0.046875
- w_key: bfloat16 [16384, 1024], P('gx', 'gy'), may hold values from -0.046875 to 0.046875
- w_value: bfloat16 [16384, 1024], P('gx', 'gy'), may hold values from -0.046875 to 0.046875
- w_out: bfloat16 [16384, 16384], P('gy', 'gx'), may hold values from -0.375 to 0.375
- w_gate: bfloat16 [16384, 26624], P('gx', 'gy'), may hold values from -0.046875 to 0.046875
- w_up: bfloat16 [16384, 26624], P('gx', 'gy'), may hold values from -0.046875 to 0.046875
- key_cache: bfloat16 [768, 128, 1024], P(('gx', 'gy')), may hold values from -1000 to 1000
- value_cache: bfloat16 [768, 128, 1024], P(('gx', 'gy')), may hold values from -6 to 6
- lengths: int32 [768], P(('gx', 'gy')), may hold values from 1 to 128, 49152 in all
Outputs:
- residual: bfloat16 [768, 16384], P('gy', 'gx')
- hidden: bfloat16 [768, 26624], P('gx', 'gy')
The draws below stay inside these ranges and needn't reach their ends.
Inputs may be any that keep to these rules, and one draw needn't show every extreme that they name: `lengths`: the longest row holds exactly 128 valid positions.
All inputs are finite; a program needn't handle non-finite values. No bound on the sum of `lengths` on one device may be relied on, other than what follows from the above.
Results may differ from the reference program's by a relative error of at most 0.04.
Values may be sent and summed in bfloat16 or wider, within the bound.
No kernel may reach another device: no remote copies, remote signals or barrier semaphores. Data moves between devices by JAX's collectives and lax.ppermute only.
A program may use at most 128 MiB of HBM per device.

```python
import math
import jax
import jax.numpy as jnp
import numpy as np
from jax import lax

D = 16384
HEADS = 128
KV_HEADS = 8
HEAD_DIM = 128
FF = 26624
CACHE = 128
ROWS = 768
Q_WIDTH = 16384
KV_WIDTH = 1024
N_GX = 8
N_GY = 16


def draw_stream(key, part):
    first_key, second_key, third_key = jax.random.split(key, 3)
    row_scales = jnp.exp(jax.random.uniform(first_key, (ROWS, 1), jnp.float32, math.log(0.3), math.log(3.0)))
    column_pos = jnp.arange(D, dtype=jnp.float32) / D
    column_scales = jnp.exp(math.log(3.0) * column_pos)[None, :] * jnp.exp(jax.random.uniform(second_key, (1, D), jnp.float32, -0.5, 0.5))
    base_values = jax.random.normal(third_key, (ROWS, D), jnp.float32)
    drawn = jnp.clip(base_values * row_scales * column_scales, -120.0, 120.0)
    return drawn.astype(jnp.bfloat16)


def draw_key_cache(key, part):
    first_key = jax.random.fold_in(key, 0)
    drawn = jax.random.normal(first_key, (ROWS, CACHE, KV_WIDTH), jnp.float32)
    return jnp.clip(drawn, -1000.0, 1000.0).astype(jnp.bfloat16)


def level_of(stream_key, extent, cuts, least, high):
    factor_of = 1.0
    for dim, parts in cuts:
        draws = jax.random.uniform(jax.random.fold_in(jax.random.fold_in(stream_key, 6), dim), (parts,), jnp.float32, least / len(cuts), high / len(cuts))
        factor_of = factor_of * jnp.repeat(jnp.exp(draws), extent[dim] // parts).reshape((-1,) + (1,) * (len(extent) - 1 - dim))
    return factor_of


def profile(amount, total, most, skew):
    portions = [(1 << 20) // math.isqrt(standing ** skew) + 1 for standing in range(2, amount + 1)]
    rest, counts = total - most - (amount - 1), [1] * (amount - 1)
    while rest > 0:
        free = [i for i in range(amount - 1) if counts[i] < most]
        mass, remaining = sum([portions[i] for i in free]), rest
        for i in free:
            more = min(most - counts[i], max(1, remaining * portions[i] // mass), rest)
            counts[i] = counts[i] + more
            rest = rest - more
    return np.array([most] + counts)


def uneven(key, count, total, limit, skew):
    if count == 2:
        one = jax.random.randint(key, (), max(1, total - limit), min(limit, total - 1) + 1)
        return jnp.stack([one, total - one])
    sizes = jnp.asarray(profile(count, total, limit, skew), jnp.int32)
    twos = (count - 1) // 2
    donor, taker = sizes[1:1 + 2 * twos:2], sizes[2:2 + 2 * twos:2]
    room = jnp.minimum(donor - 1, limit - taker)
    shifted = jax.random.randint(jax.random.fold_in(key, 1), (twos,), 0, 1 << 20) % (room + 1)
    sizes = sizes.at[1:1 + 2 * twos:2].set(donor - shifted).at[2:2 + 2 * twos:2].set(taker + shifted)
    return sizes[jax.random.permutation(jax.random.fold_in(key, 2), count)]


def normal_values(stream_key, shape, width, limit, pieces=(), kind=jnp.bfloat16):
    values = width * jax.random.normal(stream_key, shape, jnp.float32)
    if pieces:
        values = values * level_of(stream_key, shape, pieces, -0.22, 0.18)
    return jnp.clip(values, -limit, limit).astype(kind)


def setup_inputs(seed: int = 0) -> dict:
    seeds = jax.random.split(jax.random.key(seed), 13)
    return {
        "stream": draw_stream(jax.random.fold_in(seeds[12], 71), 0),
        "attn_gain": jnp.clip(1.0 + 0.18 * jax.random.normal(seeds[1], (D,), jnp.float32), 0.099609375, 1.8984375).astype(jnp.bfloat16),
        "ffn_gain": jnp.clip(1.0 + 0.18 * jax.random.normal(seeds[2], (D,), jnp.float32), 0.099609375, 1.8984375).astype(jnp.bfloat16),
        "w_query": normal_values(seeds[3], (D, Q_WIDTH), D ** -0.5, 0.046875, ((0, 8), (1, 16))),
        "w_key": normal_values(seeds[4], (D, KV_WIDTH), D ** -0.5, 0.046875, ((0, 8), (1, 16))),
        "w_value": normal_values(seeds[5], (D, KV_WIDTH), D ** -0.5, 0.046875, ((0, 8), (1, 16))),
        "w_out": normal_values(seeds[6], (Q_WIDTH, D), (2 * HEAD_DIM) ** -0.5, 0.375, ((0, 16), (1, 8))),
        "w_gate": normal_values(seeds[7], (D, FF), D ** -0.5, 0.046875, ((0, 8), (1, 16))),
        "w_up": normal_values(seeds[8], (D, FF), D ** -0.5, 0.046875, ((0, 8), (1, 16))),
        "key_cache": draw_key_cache(jax.random.fold_in(seeds[12], 71), 0),
        "value_cache": normal_values(seeds[10], (ROWS, CACHE, KV_WIDTH), 1.0, 6.0, ((0, 128),)),
        "lengths": uneven(seeds[11], ROWS, ROWS * CACHE // 2, CACHE, 2).astype(jnp.int32),
    }


epsilon = 1e-05

def rms_scale(values, gain):
    values_f = values.astype(jnp.float32)
    mean_square = lax.optimization_barrier(jnp.mean(values_f * values_f, axis=1, keepdims=True))
    return (values_f * lax.rsqrt(mean_square + epsilon) * gain.astype(jnp.float32)[None, :]).astype(jnp.bfloat16)

def blocked_product(left_side, right_side, blocks):
    block_width = left_side.shape[1] // blocks

    def add_block(block_index, running):
        offset = (jnp.asarray(block_index, jnp.int32) * block_width).astype(jnp.int32)
        left_part = lax.dynamic_slice_in_dim(left_side, offset, block_width, 1)
        right_part = lax.dynamic_slice_in_dim(right_side, offset, block_width, 0)
        product = jnp.dot(left_part, right_part, preferred_element_type=jnp.float32)
        rounded = lax.optimization_barrier(product.astype(jnp.bfloat16))
        return running + rounded.astype(jnp.float32)
    initial = jnp.zeros((left_side.shape[0], right_side.shape[1]), jnp.float32)
    return lax.fori_loop(0, blocks, add_block, initial)

def attend_row(packed):
    query_row, key_row, value_row, cached_keys, cached_values, row_length = packed
    per_group = HEADS // KV_HEADS
    score_scale = HEAD_DIM ** (-0.5)
    grouped_q = query_row.astype(jnp.float32).reshape(KV_HEADS, per_group, HEAD_DIM)
    keys_f = cached_keys.astype(jnp.float32).reshape(CACHE, KV_HEADS, HEAD_DIM)
    values_f = cached_values.astype(jnp.float32).reshape(CACHE, KV_HEADS, HEAD_DIM)
    scores = jnp.einsum('gqd,lgd->gql', grouped_q, keys_f) * score_scale
    own_score = jnp.einsum('gqd,gd->gq', grouped_q, key_row.astype(jnp.float32).reshape(KV_HEADS, HEAD_DIM)) * score_scale
    in_range = jnp.arange(CACHE) < row_length
    scores = jnp.where(in_range[None, None, :], scores, -jnp.inf)
    row_top = jnp.maximum(lax.optimization_barrier(jnp.max(scores, axis=2)), own_score)
    exp_all = jnp.exp(scores - row_top[:, :, None])
    exp_own = jnp.exp(own_score - row_top)
    denominator = lax.optimization_barrier(jnp.sum(exp_all, axis=2)) + exp_own
    weights_all = (exp_all / denominator[:, :, None]).astype(jnp.bfloat16)
    weight_own = (exp_own / denominator).astype(jnp.bfloat16)
    mixed = jnp.einsum('gql,lgd->gqd', weights_all.astype(jnp.float32), values_f)
    mixed = mixed + weight_own.astype(jnp.float32)[:, :, None] * value_row.astype(jnp.float32).reshape(KV_HEADS, 1, HEAD_DIM)
    return mixed.reshape(Q_WIDTH).astype(jnp.bfloat16)

def reference(stream, attn_gain, ffn_gain, w_query, w_key, w_value, w_out, w_gate, w_up, key_cache, value_cache, lengths):
    normed = rms_scale(stream, attn_gain)
    query = blocked_product(normed, w_query, N_GX).astype(jnp.bfloat16)
    key_new = blocked_product(normed, w_key, N_GX).astype(jnp.bfloat16)
    value_new = blocked_product(normed, w_value, N_GX).astype(jnp.bfloat16)
    heads = lax.map(attend_row, (query, key_new, value_new, key_cache, value_cache, lengths))
    attn_out = blocked_product(heads, w_out, N_GY)
    residual = (stream.astype(jnp.float32) + attn_out).astype(jnp.bfloat16)
    normed_two = rms_scale(residual, ffn_gain)
    gate = blocked_product(normed_two, w_gate, N_GX)
    up_part = blocked_product(normed_two, w_up, N_GX)
    hidden = (jax.nn.silu(gate) * up_part).astype(jnp.bfloat16)
    return (residual, hidden)
```

```python
import jax
import jax.numpy as jnp
from jax import lax
from jax.sharding import PartitionSpec as P

D = 16384
HEAD_DIM = 128
N_Y, N_C, N_Z, N_X = 4, 2, 4, 4

epsilon = 1e-05

bf16 = jnp.bfloat16
f32 = jnp.float32


def send_gy(values, dz, dx):
    pairs = []
    for z in range(N_Z):
        for x in range(N_X):
            pairs.append((z * N_X + x, ((z + dz) % N_Z) * N_X + (x + dx) % N_X))
    return lax.ppermute(values, "gy", pairs)


def send_gx(values, dy, dc):
    pairs = []
    for y in range(N_Y):
        for c in range(N_C):
            pairs.append((y * N_C + c, ((y + dy) % N_Y) * N_C + (c + dc) % N_C))
    return lax.ppermute(values, "gx", pairs)


def send_x(values, step):
    return send_gy(values, 0, step)


def send_z(values, step):
    return send_gy(values, step, 0)


def send_y(values, step):
    return send_gx(values, step, 0)


def swap_core(values):
    return send_gx(values, 0, 1)


def ring_gather(block, send):
    after = send(block, -1)
    before = send(block, 1)
    half = block.shape[-1] // 2
    far = jnp.concatenate(
        [send(after[..., :half], -1), send(before[..., half:], 1)], axis=-1
    )
    return after, far, before


def ring_reduce(pick, here, send):
    far = pick((here + 2) & 3)
    half = far.shape[-1] // 2
    after = pick((here + 1) & 3)
    before = pick((here + 3) & 3)
    got_far_low = send(far[..., :half], 1)
    got_far_high = send(far[..., half:], -1)
    got_before_high = send(after[..., half:], 1)
    got_after_low = send(before[..., :half], -1)
    low = (after[..., :half].astype(f32) + got_far_low.astype(f32)).astype(bf16)
    high = (before[..., half:].astype(f32) + got_far_high.astype(f32)).astype(bf16)
    got_before_low = send(low, 1)
    got_after_high = send(high, -1)
    own = pick(here).astype(f32)
    low_sum = own[..., :half] + got_before_low.astype(f32) + got_after_low.astype(f32)
    high_sum = own[..., half:] + got_before_high.astype(f32) + got_after_high.astype(f32)
    return jnp.concatenate([low_sum, high_sum], axis=-1)


def row_squares(values):
    values_f = values.astype(f32)
    return jnp.sum(values_f * values_f, axis=1)


def all_row_squares(partial, z, x):
    total = partial + swap_core(partial)
    total = total + send_y(total, 1) + send_y(total, -1) + send_y(total, 2)
    line = jnp.zeros((N_X,) + total.shape, f32)
    line = lax.dynamic_update_slice(line, total[None], (x, 0))
    for k in (1, 2, 3):
        line = lax.dynamic_update_slice(line, send_x(total, -k)[None], ((x + k) & 3, 0))
    plane = jnp.zeros((N_Z,) + line.shape, f32)
    plane = lax.dynamic_update_slice(plane, line[None], (z, 0, 0))
    for k in (1, 2, 3):
        plane = lax.dynamic_update_slice(plane, send_z(line, -k)[None], ((z + k) & 3, 0, 0))
    return plane


def torus_gather(block, z, x):
    rows, width = block.shape
    half = rows // 2
    out = jnp.zeros((N_Z, N_X, rows, width), block.dtype)
    first, second = block[:half], block[half:]
    after, far, before = ring_gather(first, send_x)
    line = jnp.zeros((N_X, half, width), block.dtype)
    for k, piece in ((0, first), (1, after), (3, before), (2, far)):
        line = lax.dynamic_update_slice(line, piece[None], ((x + k) & 3, 0, 0))
    after, far, before = ring_gather(line, send_z)
    for k, piece in ((0, line), (1, after), (3, before), (2, far)):
        out = lax.dynamic_update_slice(out, piece[None], ((z + k) & 3, 0, 0, 0))
    after, far, before = ring_gather(second, send_z)
    line = jnp.zeros((N_Z, half, width), block.dtype)
    for k, piece in ((0, second), (1, after), (3, before), (2, far)):
        line = lax.dynamic_update_slice(line, piece[None], ((z + k) & 3, 0, 0))
    after, far, before = ring_gather(line, send_x)
    for k, piece in ((0, line), (1, after), (3, before), (2, far)):
        out = lax.dynamic_update_slice(
            out, piece[:, None], (0, (x + k) & 3, half, 0)
        )
    return out


def attend_block(query, key_new, value_new, key_cache, value_cache, lengths):
    rows_here = query.shape[0]
    cache_len = key_cache.shape[1]
    groups = key_cache.shape[2] // HEAD_DIM
    per_group = query.shape[1] // key_cache.shape[2]
    score_scale = HEAD_DIM ** (-0.5)
    grouped_q = query.reshape(rows_here, groups, per_group, HEAD_DIM)
    cached_keys = key_cache.reshape(rows_here, cache_len, groups, HEAD_DIM)
    cached_values = value_cache.reshape(rows_here, cache_len, groups, HEAD_DIM)
    scores = (
        jnp.einsum("rgqd,rlgd->rgql", grouped_q, cached_keys, preferred_element_type=f32)
        * score_scale
    )
    own_score = (
        jnp.einsum(
            "rgqd,rgd->rgq",
            grouped_q,
            key_new.reshape(rows_here, groups, HEAD_DIM),
            preferred_element_type=f32,
        )
        * score_scale
    )
    in_range = jnp.arange(cache_len)[None, :] < lengths[:, None]
    scores = jnp.where(in_range[:, None, None, :], scores, -jnp.inf)
    row_top = jnp.maximum(jnp.max(scores, axis=3), own_score)
    exp_all = jnp.exp(scores - row_top[:, :, :, None])
    exp_own = jnp.exp(own_score - row_top)
    denominator = jnp.sum(exp_all, axis=3) + exp_own
    weights_all = (exp_all / denominator[:, :, :, None]).astype(bf16)
    weight_own = (exp_own / denominator).astype(bf16)
    mixed = jnp.einsum("rgql,rlgd->rgqd", weights_all, cached_values, preferred_element_type=f32)
    own_values = value_new.astype(f32).reshape(rows_here, groups, 1, HEAD_DIM)
    mixed = mixed + weight_own.astype(f32)[:, :, :, None] * own_values
    return mixed.reshape(rows_here, per_group * groups * HEAD_DIM).astype(bf16)


def on_device(
    stream,
    attn_gain,
    ffn_gain,
    w_query,
    w_key,
    w_value,
    w_out,
    w_gate,
    w_up,
    key_cache,
    value_cache,
    lengths,
):
    rows_dev = key_cache.shape[0]
    size_gy = lax.axis_size("gy")
    rows_j = stream.shape[0]
    rows_i = 2 * rows_j
    gx, gy = lax.axis_index("gx"), lax.axis_index("gy")
    y, c = gx >> 1, gx & 1
    z, x = gy >> 2, gy & 3
    query_cols = w_query.shape[1]
    key_cols = w_key.shape[1]

    squares = all_row_squares(row_squares(stream), z, x).reshape(N_Y * N_C, rows_i)
    gained = (stream.astype(f32) * attn_gain.astype(f32)[None, :]).astype(bf16)
    features = torus_gather(gained, z, x)
    by_core = features.reshape(N_Y, N_C, rows_i, features.shape[-1])
    w_kv = jnp.concatenate([w_key, w_value], axis=1)

    def qkv_rows(core):
        block = lax.dynamic_slice_in_dim(by_core, core, 1, axis=1).reshape(N_Y * rows_i, -1)
        return [
            jnp.dot(block, w_query, preferred_element_type=f32).astype(bf16),
            jnp.dot(block, w_kv, preferred_element_type=f32).astype(bf16),
        ]

    other = jnp.concatenate(qkv_rows(1 - c), axis=1)
    other = swap_core(other).astype(f32)
    mine = jnp.concatenate(qkv_rows(c), axis=1).astype(f32)
    mine = (mine + other).astype(bf16).reshape(N_Y, rows_i, -1)

    def pick(k):
        return lax.dynamic_index_in_dim(mine, k, 0, keepdims=False)

    summed = ring_reduce(pick, y, send_y)
    inverse = lax.rsqrt(squares / D + epsilon)
    inverse_here = lax.dynamic_index_in_dim(inverse, gx, 0, keepdims=False)
    summed = (summed * inverse_here[:, None]).astype(bf16)

    combined = lax.all_to_all(summed, "gy", split_axis=0, concat_axis=1, tiled=True)
    col_count = query_cols + 2 * key_cols
    blocks = combined.reshape(rows_dev, size_gy, col_count)
    query = blocks[:, :, :query_cols].reshape(rows_dev, size_gy * query_cols)
    key_new = blocks[:, :, query_cols : query_cols + key_cols].reshape(rows_dev, size_gy * key_cols)
    value_new = blocks[:, :, query_cols + key_cols :].reshape(rows_dev, size_gy * key_cols)
    heads = attend_block(query, key_new, value_new, key_cache, value_cache, lengths)
    heads_moved = lax.all_to_all(heads, "gy", split_axis=1, concat_axis=0, tiled=True)

    after, far, before = ring_gather(heads_moved, send_y)
    head_rows = jnp.zeros((N_Y, N_C, rows_i, heads_moved.shape[1]), bf16)
    for k, piece in ((0, heads_moved), (1, after), (3, before), (2, far)):
        row = (y + k) & 3
        head_rows = lax.dynamic_update_slice(head_rows, piece[None, None], (row, c, 0, 0))
        head_rows = lax.dynamic_update_slice(
            head_rows, swap_core(piece)[None, None], (row, 1 - c, 0, 0)
        )
    head_rows = head_rows.reshape(N_Z, N_X, rows_j, -1)

    half = w_out.shape[1] // 2

    def low_part(k):
        block = lax.dynamic_slice_in_dim(head_rows, k, 1, axis=1).reshape(N_Z * rows_j, -1)
        return jnp.dot(block, w_out[:, :half], preferred_element_type=f32).astype(bf16)

    def high_part(k):
        block = lax.dynamic_slice_in_dim(head_rows, k, 1, axis=0).reshape(N_X * rows_j, -1)
        return jnp.dot(block, w_out[:, half:], preferred_element_type=f32).astype(bf16)

    low = ring_reduce(low_part, x, send_x).astype(bf16).reshape(N_Z, rows_j, half)
    high = ring_reduce(high_part, z, send_z).astype(bf16).reshape(N_X, rows_j, half)
    low = ring_reduce(
        lambda k: lax.dynamic_index_in_dim(low, k, 0, keepdims=False), z, send_z
    )
    high = ring_reduce(
        lambda k: lax.dynamic_index_in_dim(high, k, 0, keepdims=False), x, send_x
    )
    attn_share = jnp.concatenate([low, high], axis=1)
    residual = (stream.astype(f32) + attn_share).astype(bf16)

    squares_two = all_row_squares(row_squares(residual), z, x).reshape(N_Y * N_C, rows_i)
    gained_two = (residual.astype(f32) * ffn_gain.astype(f32)[None, :]).astype(bf16)
    features_two = torus_gather(gained_two, z, x)
    by_core_two = features_two.reshape(N_Y, N_C, rows_i, features_two.shape[-1])
    inverse_two = lax.rsqrt(squares_two / D + epsilon)
    inverse_two = lax.dynamic_index_in_dim(inverse_two, gx, 0, keepdims=False)

    def reduced(weight):
        def rows_of(core):
            block = lax.dynamic_slice_in_dim(by_core_two, core, 1, axis=1)
            block = block.reshape(N_Y * rows_i, -1)
            return jnp.dot(block, weight, preferred_element_type=f32)

        other = swap_core(rows_of(1 - c).astype(bf16)).astype(f32)
        mine = (rows_of(c) + other).astype(bf16).reshape(N_Y, rows_i, -1)
        total = ring_reduce(
            lambda k: lax.dynamic_index_in_dim(mine, k, 0, keepdims=False), y, send_y
        )
        return total * inverse_two[:, None]

    gate = reduced(w_gate)
    up = reduced(w_up)
    hidden = (jax.nn.silu(gate) * up).astype(bf16)
    return (residual, hidden)


def solution(mesh):
    placed = (
        P("gy", "gx"),
        P("gx"),
        P("gx"),
        P("gx", "gy"),
        P("gx", "gy"),
        P("gx", "gy"),
        P("gy", "gx"),
        P("gx", "gy"),
        P("gx", "gy"),
        P(("gx", "gy"), None, None),
        P(("gx", "gy"), None, None),
        P(("gx", "gy")),
    )
    return jax.shard_map(
        on_device,
        mesh=mesh,
        in_specs=placed,
        out_specs=(P("gy", "gx"), P("gx", "gy")),
        check_vma=False,
    )
```

```python
import jax
import jax.numpy as jnp
from jax import lax
from jax.sharding import PartitionSpec as P

D = 16384
HEAD_DIM = 128
N_Y, N_C, N_Z, N_X = 4, 2, 4, 4
LANES = 128

epsilon = 1e-05

bf16 = jnp.bfloat16
f32 = jnp.float32


def send_gy(values, dz, dx):
    pairs = []
    for z in range(N_Z):
        for x in range(N_X):
            pairs.append((z * N_X + x, ((z + dz) % N_Z) * N_X + (x + dx) % N_X))
    return lax.ppermute(values, "gy", pairs)


def send_gx(values, dy, dc):
    pairs = []
    for y in range(N_Y):
        for c in range(N_C):
            pairs.append((y * N_C + c, ((y + dy) % N_Y) * N_C + (c + dc) % N_C))
    return lax.ppermute(values, "gx", pairs)


def send_x(values, step):
    return send_gy(values, 0, step)


def send_z(values, step):
    return send_gy(values, step, 0)


def send_y(values, step):
    return send_gx(values, step, 0)


def swap_core(values):
    return send_gx(values, 0, 1)


def ring_gather(block, send, direct):
    if direct:
        return send(block, -1), send(block, 2), send(block, 1)
    after = send(block, -1)
    before = send(block, 1)
    half = block.shape[-1] // 2
    far = jnp.concatenate(
        [send(after[..., :half], -1), send(before[..., half:], 1)], axis=-1
    )
    return after, far, before


def ring_reduce(far, after, before, own, send, step):
    near, other = (after, before) if step == 1 else (before, after)
    got_far = send(far, step)
    got_other = send(other, -step)
    near = (near.astype(f32) + got_far.astype(f32)).astype(bf16)
    got_near = send(near, step)
    return own.astype(f32) + got_other.astype(f32) + got_near.astype(f32)


def ring_reduce_split(far, after, before, own, send, cut):
    got_low = send(far[..., :cut], 1)
    got_high = send(far[..., cut:], -1)
    low = (after[..., :cut].astype(f32) + got_low.astype(f32)).astype(bf16)
    high = (before[..., cut:].astype(f32) + got_high.astype(f32)).astype(bf16)
    got_before = send(jnp.concatenate([low, after[..., cut:]], axis=-1), 1)
    got_after = send(jnp.concatenate([before[..., :cut], high], axis=-1), -1)
    return own.astype(f32) + got_before.astype(f32) + got_after.astype(f32)


def squares_columns(values, gx):
    values_f = values.astype(f32)
    total = jnp.sum(values_f * values_f, axis=-1)
    high = lax.reduce_precision(total, 8, 7)
    rest = total - high
    middle = lax.reduce_precision(rest, 8, 7)
    low = rest - middle
    lane = lax.broadcasted_iota(jnp.int32, total.shape + (LANES,), total.ndim)
    columns = jnp.where(lane == gx, high[..., None], 0.0)
    columns = jnp.where(lane == gx + 8, middle[..., None], columns)
    columns = jnp.where(lane == gx + 16, low[..., None], columns)
    return columns.astype(bf16)


def row_inverse(columns):
    return lax.rsqrt(jnp.sum(columns, axis=1, keepdims=True) / D + epsilon)


def torus_gather(block, z, x):
    rows, width = block.shape
    half = rows // 2
    out = jnp.zeros((N_Z, N_X, rows, width), block.dtype)
    first, second = block[:half], block[half:]
    after, far, before = ring_gather(first, send_x, True)
    line = jnp.zeros((N_X, half, width), block.dtype)
    for k, piece in ((0, first), (1, after), (3, before), (2, far)):
        line = lax.dynamic_update_slice(line, piece[None], ((x + k) & 3, 0, 0))
    after, far, before = ring_gather(second, send_z, True)
    line_two = jnp.zeros((N_Z, half, width), block.dtype)
    for k, piece in ((0, second), (1, after), (3, before), (2, far)):
        line_two = lax.dynamic_update_slice(line_two, piece[None], ((z + k) & 3, 0, 0))
    after, far, before = ring_gather(line, send_z, False)
    for k, piece in ((0, line), (1, after), (3, before), (2, far)):
        out = lax.dynamic_update_slice(out, piece[None], ((z + k) & 3, 0, 0, 0))
    after, far, before = ring_gather(line_two, send_x, False)
    for k, piece in ((0, line_two), (1, after), (3, before), (2, far)):
        out = lax.dynamic_update_slice(out, piece[:, None], (0, (x + k) & 3, half, 0))
    return out


def attend_block(query, key_new, value_new, key_cache, value_cache, lengths):
    rows_here = query.shape[0]
    cache_len = key_cache.shape[1]
    groups = key_cache.shape[2] // HEAD_DIM
    per_group = query.shape[1] // key_cache.shape[2]
    score_scale = HEAD_DIM ** (-0.5)
    grouped_q = query.reshape(rows_here, groups, per_group, HEAD_DIM)
    cached_keys = key_cache.reshape(rows_here, cache_len, groups, HEAD_DIM)
    cached_values = value_cache.reshape(rows_here, cache_len, groups, HEAD_DIM)
    scores = (
        jnp.einsum("rgqd,rlgd->rgql", grouped_q, cached_keys, preferred_element_type=f32)
        * score_scale
    )
    own_score = (
        jnp.einsum(
            "rgqd,rgd->rgq",
            grouped_q,
            key_new.reshape(rows_here, groups, HEAD_DIM),
            preferred_element_type=f32,
        )
        * score_scale
    )
    in_range = jnp.arange(cache_len)[None, :] < lengths[:, None]
    scores = jnp.where(in_range[:, None, None, :], scores, -jnp.inf)
    row_top = jnp.maximum(jnp.max(scores, axis=3), own_score)
    exp_all = jnp.exp(scores - row_top[:, :, :, None])
    exp_own = jnp.exp(own_score - row_top)
    denominator = jnp.sum(exp_all, axis=3) + exp_own
    weights_all = (exp_all / denominator[:, :, :, None]).astype(bf16)
    weight_own = (exp_own / denominator).astype(bf16)
    mixed = jnp.einsum("rgql,rlgd->rgqd", weights_all, cached_values, preferred_element_type=f32)
    own_values = value_new.astype(f32).reshape(rows_here, groups, 1, HEAD_DIM)
    mixed = mixed + weight_own.astype(f32)[:, :, :, None] * own_values
    return mixed.reshape(rows_here, per_group * groups * HEAD_DIM).astype(bf16)


def on_device(
    stream,
    attn_gain,
    ffn_gain,
    w_query,
    w_key,
    w_value,
    w_out,
    w_gate,
    w_up,
    key_cache,
    value_cache,
    lengths,
):
    rows_dev = key_cache.shape[0]
    size_gy = lax.axis_size("gy")
    rows_j = stream.shape[0]
    rows_i = 2 * rows_j
    gx, gy = lax.axis_index("gx"), lax.axis_index("gy")
    y, c = gx >> 1, gx & 1
    z, x = gy >> 2, gy & 3
    query_cols = w_query.shape[1]
    key_cols = w_key.shape[1]

    features = torus_gather(stream, z, x)
    by_core = features.reshape(N_Y, N_C, rows_i, features.shape[-1])
    w_kv = jnp.concatenate([w_key, w_value], axis=1)
    attn_gain_f = attn_gain.astype(f32)[None, :]

    def qkv_rows(core):
        raw = lax.dynamic_slice_in_dim(by_core, core, 1, axis=1).reshape(N_Y * rows_i, -1)
        block = (raw.astype(f32) * attn_gain_f).astype(bf16)
        return jnp.concatenate(
            [
                jnp.dot(block, w_query, preferred_element_type=f32).astype(bf16),
                jnp.dot(block, w_kv, preferred_element_type=f32).astype(bf16),
                squares_columns(raw, gx),
            ],
            axis=1,
        )

    other = swap_core(qkv_rows(1 - c)).astype(f32)
    mine = (qkv_rows(c).astype(f32) + other).astype(bf16).reshape(N_Y, rows_i, -1)

    def at(k):
        return lax.dynamic_index_in_dim(mine, (y + k) & 3, 0, keepdims=False)

    col_count = query_cols + 2 * key_cols
    summed = ring_reduce_split(at(2), at(1), at(3), at(0), send_y, query_cols // 2 + LANES)
    summed = (summed[:, :col_count] * row_inverse(summed[:, col_count:])).astype(bf16)

    combined = lax.all_to_all(summed, "gy", split_axis=0, concat_axis=1, tiled=True)
    blocks = combined.reshape(rows_dev, size_gy, col_count)
    query = blocks[:, :, :query_cols].reshape(rows_dev, size_gy * query_cols)
    key_new = blocks[:, :, query_cols : query_cols + key_cols].reshape(rows_dev, size_gy * key_cols)
    value_new = blocks[:, :, query_cols + key_cols :].reshape(rows_dev, size_gy * key_cols)
    heads = attend_block(query, key_new, value_new, key_cache, value_cache, lengths)
    heads_moved = lax.all_to_all(heads, "gy", split_axis=1, concat_axis=0, tiled=True)

    after = send_y(heads_moved, -1)
    before = send_y(heads_moved, 1)
    far = send_y(before, 1)
    line = jnp.zeros((N_Y,) + heads_moved.shape, bf16)
    for k, piece in ((0, heads_moved), (1, after), (3, before), (2, far)):
        line = lax.dynamic_update_slice(line, piece[None], ((y + k) & 3, 0, 0))
    head_rows = jnp.zeros((N_Y, N_C, rows_i, heads_moved.shape[1]), bf16)
    head_rows = lax.dynamic_update_slice(head_rows, line[:, None], (0, c, 0, 0))
    head_rows = lax.dynamic_update_slice(head_rows, swap_core(line)[:, None], (0, 1 - c, 0, 0))
    head_rows = head_rows.reshape(N_Z, N_X, rows_j, -1)

    half = w_out.shape[1] // 2

    def low_part(k):
        block = lax.dynamic_slice_in_dim(head_rows, k, 1, axis=1).reshape(N_Z * rows_j, -1)
        return jnp.dot(block, w_out[:, :half], preferred_element_type=f32).astype(bf16)

    def high_part(k):
        block = lax.dynamic_slice_in_dim(head_rows, k, 1, axis=0).reshape(N_X * rows_j, -1)
        return jnp.dot(block, w_out[:, half:], preferred_element_type=f32).astype(bf16)

    def reduced(part, here, send, step):
        terms = [part((here + k) & 3) for k in (2, 1, 3, 0)]
        return ring_reduce(*terms, send, step)

    low = reduced(low_part, x, send_x, 1).astype(bf16).reshape(N_Z, rows_j, half)
    high = reduced(high_part, z, send_z, -1).astype(bf16).reshape(N_X, rows_j, half)
    low = reduced(lambda k: lax.dynamic_index_in_dim(low, k, 0, keepdims=False), z, send_z, -1)
    high = reduced(lambda k: lax.dynamic_index_in_dim(high, k, 0, keepdims=False), x, send_x, 1)
    attn_share = jnp.concatenate([low, high], axis=1)
    residual = (stream.astype(f32) + attn_share).astype(bf16)

    features_two = torus_gather(residual, z, x)
    gained_two = features_two.astype(f32) * ffn_gain.astype(f32)[None, None, None, :]
    gained_two = gained_two.astype(bf16).reshape(N_Y, N_C, rows_i, -1)
    squares_two = squares_columns(features_two, gx).reshape(N_Y, N_C, rows_i, LANES)

    def take(places):
        def rows(array):
            pieces = [
                lax.dynamic_slice(array, (at_y, at_c, 0, 0), (1, 1) + array.shape[2:])[0, 0]
                for at_y, at_c in places
            ]
            return jnp.concatenate(pieces, axis=0)

        block = rows(gained_two)
        out = jnp.concatenate(
            [
                jnp.dot(block, w_gate, preferred_element_type=f32).astype(bf16),
                jnp.dot(block, w_up, preferred_element_type=f32).astype(bf16),
                rows(squares_two),
            ],
            axis=1,
        )
        return out.reshape(len(places), rows_i, -1)

    def with_other(theirs, ours):
        return (ours.astype(f32) + swap_core(theirs).astype(f32)).astype(bf16)

    y_far, y_after, y_before = (y + 2) & 3, (y + 1) & 3, (y + 3) & 3
    far = take([(y_far, 1 - c), (y_far, c)])
    far = with_other(far[0], far[1])
    near_theirs = take([(y_after, 1 - c), (y_before, 1 - c)])
    near_ours = take([(y_after, c), (y_before, c)])
    near = with_other(near_theirs, near_ours)
    own = take([(y, 1 - c), (y, c)])
    own = with_other(own[0], own[1])
    split_at = w_gate.shape[1]
    gate_up = ring_reduce_split(far, near[0], near[1], own, send_y, split_at)
    inverse_two = row_inverse(gate_up[:, 2 * split_at :])
    gate = gate_up[:, :split_at] * inverse_two
    up = gate_up[:, split_at : 2 * split_at] * inverse_two
    hidden = (jax.nn.silu(gate) * up).astype(bf16)
    return (residual, hidden)


def solution(mesh):
    placed = (
        P("gy", "gx"),
        P("gx"),
        P("gx"),
        P("gx", "gy"),
        P("gx", "gy"),
        P("gx", "gy"),
        P("gy", "gx"),
        P("gx", "gy"),
        P("gx", "gy"),
        P(("gx", "gy"), None, None),
        P(("gx", "gy"), None, None),
        P(("gx", "gy")),
    )
    return jax.shard_map(
        on_device,
        mesh=mesh,
        in_specs=placed,
        out_specs=(P("gy", "gx"), P("gx", "gy")),
        check_vma=False,
    )
```

```python
import jax
import jax.numpy as jnp
from jax import lax
from jax.sharding import PartitionSpec as P

D = 16384
HEAD_DIM = 128
N_Y, N_C, N_Z, N_X = 4, 2, 4, 4
LANES = 128

epsilon = 1e-05

bf16 = jnp.bfloat16
f32 = jnp.float32


def send_gy(values, dz, dx):
    pairs = []
    for z in range(N_Z):
        for x in range(N_X):
            pairs.append((z * N_X + x, ((z + dz) % N_Z) * N_X + (x + dx) % N_X))
    return lax.ppermute(values, "gy", pairs)


def send_gx(values, dy, dc):
    pairs = []
    for y in range(N_Y):
        for c in range(N_C):
            pairs.append((y * N_C + c, ((y + dy) % N_Y) * N_C + (c + dc) % N_C))
    return lax.ppermute(values, "gx", pairs)


def send_x(values, step):
    return send_gy(values, 0, step)


def send_z(values, step):
    return send_gy(values, step, 0)


def send_y(values, step):
    return send_gx(values, step, 0)


def swap_core(values):
    return send_gx(values, 0, 1)


def ring_gather(block, send, direct):
    if direct:
        return send(block, -1), send(block, 2), send(block, 1)
    after = send(block, -1)
    before = send(block, 1)
    half = block.shape[-1] // 2
    far = jnp.concatenate(
        [send(after[..., :half], -1), send(before[..., half:], 1)], axis=-1
    )
    return after, far, before


def ring_reduce(far, after, before, own, send, step):
    near, other = (after, before) if step == 1 else (before, after)
    got_far = send(far, step)
    got_other = send(other, -step)
    near = (near.astype(f32) + got_far.astype(f32)).astype(bf16)
    got_near = send(near, step)
    return own.astype(f32) + got_other.astype(f32) + got_near.astype(f32)


def squares_columns(values, gx):
    values_f = values.astype(f32)
    total = jnp.sum(values_f * values_f, axis=-1)
    high = lax.reduce_precision(total, 8, 7)
    rest = total - high
    middle = lax.reduce_precision(rest, 8, 7)
    low = rest - middle
    lane = lax.broadcasted_iota(jnp.int32, total.shape + (LANES,), total.ndim)
    columns = jnp.where(lane == gx, high[..., None], 0.0)
    columns = jnp.where(lane == gx + 8, middle[..., None], columns)
    columns = jnp.where(lane == gx + 16, low[..., None], columns)
    return columns.astype(bf16)


def row_inverse(columns):
    return lax.rsqrt(jnp.sum(columns, axis=1, keepdims=True) / D + epsilon)


def torus_gather(block, z, x):
    rows, width = block.shape
    half = rows // 2
    out = jnp.zeros((N_Z, N_X, rows, width), block.dtype)
    first, second = block[:half], block[half:]
    after, far, before = ring_gather(first, send_x, True)
    line = jnp.zeros((N_X, half, width), block.dtype)
    for k, piece in ((0, first), (1, after), (3, before), (2, far)):
        line = lax.dynamic_update_slice(line, piece[None], ((x + k) & 3, 0, 0))
    after, far, before = ring_gather(second, send_z, True)
    line_two = jnp.zeros((N_Z, half, width), block.dtype)
    for k, piece in ((0, second), (1, after), (3, before), (2, far)):
        line_two = lax.dynamic_update_slice(line_two, piece[None], ((z + k) & 3, 0, 0))
    after, far, before = ring_gather(line, send_z, False)
    for k, piece in ((0, line), (1, after), (3, before), (2, far)):
        out = lax.dynamic_update_slice(out, piece[None], ((z + k) & 3, 0, 0, 0))
    after, far, before = ring_gather(line_two, send_x, False)
    for k, piece in ((0, line_two), (1, after), (3, before), (2, far)):
        out = lax.dynamic_update_slice(out, piece[:, None], (0, (x + k) & 3, half, 0))
    return out


def with_squares(features, gain, gx):
    gained = features.astype(f32) * gain.astype(f32)[None, None, None, :]
    by_core = (N_Y, N_C, N_X * features.shape[2] // N_C, -1)
    return gained.astype(bf16).reshape(by_core), squares_columns(features, gx).reshape(by_core)


def products_reduced(gained, squares, weights, y, c, cut):
    y_far, y_after, y_before = (y + 2) & 3, (y + 1) & 3, (y + 3) & 3

    def rows(array, places):
        pieces = [
            lax.dynamic_slice(array, (at_y, at_c, 0, 0), (1, 1) + array.shape[2:])[0, 0]
            for at_y, at_c in places
        ]
        return jnp.concatenate(pieces, axis=0)

    def products(places, ahead=None):
        block = rows(gained, places)
        if ahead is not None:
            block, _ = lax.optimization_barrier((block, ahead))
        parts = [jnp.dot(block, w, preferred_element_type=f32).astype(bf16) for w in weights]
        out = jnp.concatenate(parts + [rows(squares, places)], axis=1)
        return out.reshape(len(places), gained.shape[2], -1)

    def plus(ours, theirs):
        return (ours.astype(f32) + theirs.astype(f32)).astype(bf16)

    far = products([(y_far, 1 - c), (y_far, c)])
    theirs = products([(y_after, 1 - c), (y_before, 1 - c), (y, 1 - c)], far)
    far_sum = plus(far[1], swap_core(far[0]))
    got_low = send_y(far_sum[:, :cut], 1)
    got_high = send_y(far_sum[:, cut:], -1)
    theirs_then, _ = lax.optimization_barrier((theirs, far_sum))
    swapped = swap_core(theirs_then)
    ours = products([(y_after, c), (y_before, c)], (far_sum, theirs))
    near = plus(ours, swapped[:2])
    after = jnp.concatenate([plus(near[0, :, :cut], got_low), near[0, :, cut:]], axis=1)
    before = jnp.concatenate([near[1, :, :cut], plus(near[1, :, cut:], got_high)], axis=1)
    own = products([(y, c)], (after, before))[0]
    total = own.astype(f32) + swapped[2].astype(f32)
    return total + send_y(after, 1).astype(f32) + send_y(before, -1).astype(f32)


def attend_block(query, key_new, value_new, key_cache, value_cache, lengths):
    rows_here = query.shape[0]
    cache_len = key_cache.shape[1]
    groups = key_cache.shape[2] // HEAD_DIM
    per_group = query.shape[1] // key_cache.shape[2]
    score_scale = HEAD_DIM ** (-0.5)
    grouped_q = query.reshape(rows_here, groups, per_group, HEAD_DIM)
    cached_keys = key_cache.reshape(rows_here, cache_len, groups, HEAD_DIM)
    cached_values = value_cache.reshape(rows_here, cache_len, groups, HEAD_DIM)
    scores = (
        jnp.einsum("rgqd,rlgd->rgql", grouped_q, cached_keys, preferred_element_type=f32)
        * score_scale
    )
    own_score = (
        jnp.einsum(
            "rgqd,rgd->rgq",
            grouped_q,
            key_new.reshape(rows_here, groups, HEAD_DIM),
            preferred_element_type=f32,
        )
        * score_scale
    )
    in_range = jnp.arange(cache_len)[None, :] < lengths[:, None]
    scores = jnp.where(in_range[:, None, None, :], scores, -jnp.inf)
    row_top = jnp.maximum(jnp.max(scores, axis=3), own_score)
    exp_all = jnp.exp(scores - row_top[:, :, :, None])
    exp_own = jnp.exp(own_score - row_top)
    denominator = jnp.sum(exp_all, axis=3) + exp_own
    weights_all = (exp_all / denominator[:, :, :, None]).astype(bf16)
    weight_own = (exp_own / denominator).astype(bf16)
    mixed = jnp.einsum("rgql,rlgd->rgqd", weights_all, cached_values, preferred_element_type=f32)
    own_values = value_new.astype(f32).reshape(rows_here, groups, 1, HEAD_DIM)
    mixed = mixed + weight_own.astype(f32)[:, :, :, None] * own_values
    return mixed.reshape(rows_here, per_group * groups * HEAD_DIM).astype(bf16)


def on_device(
    stream,
    attn_gain,
    ffn_gain,
    w_query,
    w_key,
    w_value,
    w_out,
    w_gate,
    w_up,
    key_cache,
    value_cache,
    lengths,
):
    rows_dev = key_cache.shape[0]
    size_gy = lax.axis_size("gy")
    rows_j = stream.shape[0]
    rows_i = 2 * rows_j
    gx, gy = lax.axis_index("gx"), lax.axis_index("gy")
    y, c = gx >> 1, gx & 1
    z, x = gy >> 2, gy & 3
    query_cols = w_query.shape[1]
    key_cols = w_key.shape[1]

    features = torus_gather(stream, z, x)
    w_kv = jnp.concatenate([w_key, w_value], axis=1)
    col_count = query_cols + 2 * key_cols
    summed = products_reduced(
        *with_squares(features, attn_gain, gx), [w_query, w_kv], y, c, query_cols // 2 + LANES
    )
    summed = (summed[:, :col_count] * row_inverse(summed[:, col_count:])).astype(bf16)

    combined = lax.all_to_all(summed, "gy", split_axis=0, concat_axis=1, tiled=True)
    blocks = combined.reshape(rows_dev, size_gy, col_count)
    query = blocks[:, :, :query_cols].reshape(rows_dev, size_gy * query_cols)
    key_new = blocks[:, :, query_cols : query_cols + key_cols].reshape(rows_dev, size_gy * key_cols)
    value_new = blocks[:, :, query_cols + key_cols :].reshape(rows_dev, size_gy * key_cols)
    heads = attend_block(query, key_new, value_new, key_cache, value_cache, lengths)
    heads_moved = lax.all_to_all(heads, "gy", split_axis=1, concat_axis=0, tiled=True)

    after = send_y(heads_moved, -1)
    before = send_y(heads_moved, 1)
    far = send_y(before, 1)
    line = jnp.zeros((N_Y,) + heads_moved.shape, bf16)
    for k, piece in ((0, heads_moved), (1, after), (3, before), (2, far)):
        line = lax.dynamic_update_slice(line, piece[None], ((y + k) & 3, 0, 0))
    head_rows = jnp.zeros((N_Y, N_C, rows_i, heads_moved.shape[1]), bf16)
    head_rows = lax.dynamic_update_slice(head_rows, line[:, None], (0, c, 0, 0))
    head_rows = lax.dynamic_update_slice(head_rows, swap_core(line)[:, None], (0, 1 - c, 0, 0))
    head_rows = head_rows.reshape(N_Z, N_X, rows_j, -1)

    half = w_out.shape[1] // 2

    def low_part(k):
        block = lax.dynamic_slice_in_dim(head_rows, k, 1, axis=1).reshape(N_Z * rows_j, -1)
        return jnp.dot(block, w_out[:, :half], preferred_element_type=f32).astype(bf16)

    def high_part(k):
        block = lax.dynamic_slice_in_dim(head_rows, k, 1, axis=0).reshape(N_X * rows_j, -1)
        return jnp.dot(block, w_out[:, half:], preferred_element_type=f32).astype(bf16)

    def reduced(part, here, send, step):
        terms = [part((here + k) & 3) for k in (2, 1, 3, 0)]
        return ring_reduce(*terms, send, step)

    low = reduced(low_part, x, send_x, 1).astype(bf16).reshape(N_Z, rows_j, half)
    high = reduced(high_part, z, send_z, -1).astype(bf16).reshape(N_X, rows_j, half)
    low = reduced(lambda k: lax.dynamic_index_in_dim(low, k, 0, keepdims=False), z, send_z, -1)
    high = reduced(lambda k: lax.dynamic_index_in_dim(high, k, 0, keepdims=False), x, send_x, 1)
    attn_share = jnp.concatenate([low, high], axis=1)
    residual = (stream.astype(f32) + attn_share).astype(bf16)

    features_two = torus_gather(residual, z, x)
    split_at = w_gate.shape[1]
    gate_up = products_reduced(
        *with_squares(features_two, ffn_gain, gx), [w_gate, w_up], y, c, split_at
    )
    inverse_two = row_inverse(gate_up[:, 2 * split_at :])
    gate = gate_up[:, :split_at] * inverse_two
    up = gate_up[:, split_at : 2 * split_at] * inverse_two
    hidden = (jax.nn.silu(gate) * up).astype(bf16)
    return (residual, hidden)


def solution(mesh):
    placed = (
        P("gy", "gx"),
        P("gx"),
        P("gx"),
        P("gx", "gy"),
        P("gx", "gy"),
        P("gx", "gy"),
        P("gy", "gx"),
        P("gx", "gy"),
        P("gx", "gy"),
        P(("gx", "gy"), None, None),
        P(("gx", "gy"), None, None),
        P(("gx", "gy")),
    )
    return jax.shard_map(
        on_device,
        mesh=mesh,
        in_specs=placed,
        out_specs=(P("gy", "gx"), P("gx", "gy")),
        check_vma=False,
    )
```

```python
import jax
import jax.numpy as jnp
from jax import lax
from jax.sharding import PartitionSpec as P

D = 16384
HEAD_DIM = 128
N_Y, N_C, N_Z, N_X = 4, 2, 4, 4
LANES = 128

epsilon = 1e-05

bf16 = jnp.bfloat16
f32 = jnp.float32


def send_gx(values, dy, dc):
    pairs = []
    for y in range(N_Y):
        for c in range(N_C):
            pairs.append((y * N_C + c, ((y + dy) % N_Y) * N_C + (c + dc) % N_C))
    return lax.ppermute(values, "gx", pairs)


def send_first(values, step):
    return send_plane(values, step, 0)


def send_second(values, step):
    return send_plane(values, step, 1)


def send_plane(values, step, turn):
    pairs = []
    for gx in range(N_Y * N_C):
        for z in range(N_Z):
            for x in range(N_X):
                along_z = (gx + turn) % N_C
                to_z = (z + step * along_z) % N_Z
                to_x = (x + step * (1 - along_z)) % N_X
                pairs.append(((gx * N_Z + z) * N_X + x, (gx * N_Z + to_z) * N_X + to_x))
    return lax.ppermute(values, ("gx", "gy"), pairs)


def send_y(values, step):
    return send_gx(values, step, 0)


def swap_core(values):
    return send_gx(values, 0, 1)


def ring_place(block, after, far, before, here):
    out = jnp.zeros((4,) + block.shape, block.dtype)
    for k, piece in ((0, block), (1, after), (3, before), (2, far)):
        start = ((here + k) & 3,) + (0,) * block.ndim
        out = lax.dynamic_update_slice(out, piece[None], start)
    return out


def ring_reduce(far, after, before, own, send):
    cut = far.shape[-1] // 2
    got_low = send(far[..., :cut], 1)
    got_high = send(far[..., cut:], -1)
    low = (after[..., :cut].astype(f32) + got_low.astype(f32)).astype(bf16)
    high = (before[..., cut:].astype(f32) + got_high.astype(f32)).astype(bf16)
    got_before = send(jnp.concatenate([low, after[..., cut:]], axis=-1), 1)
    got_after = send(jnp.concatenate([before[..., :cut], high], axis=-1), -1)
    return own.astype(f32) + got_before.astype(f32) + got_after.astype(f32)


def squares_columns(values, gx):
    values_f = values.astype(f32)
    total = jnp.sum(values_f * values_f, axis=-1)
    high = lax.reduce_precision(total, 8, 7)
    rest = total - high
    middle = lax.reduce_precision(rest, 8, 7)
    low = rest - middle
    lane = lax.broadcasted_iota(jnp.int32, total.shape + (LANES,), total.ndim)
    columns = jnp.where(lane == gx, high[..., None], 0.0)
    columns = jnp.where(lane == gx + 8, middle[..., None], columns)
    columns = jnp.where(lane == gx + 16, low[..., None], columns)
    return columns.astype(bf16)


def row_inverse(columns):
    return lax.rsqrt(jnp.sum(columns, axis=1, keepdims=True) / D + epsilon)


def plane_gather(block, first, second):
    far, after, before = send_first(block, 2), send_first(block, -1), send_first(block, 1)
    line = ring_place(block, after, far, before, first)
    after, before = send_second(line, -1), send_second(line, 1)
    cut = block.shape[-1] // 2
    far = jnp.concatenate(
        [send_second(after[..., :cut], -1), send_second(before[..., cut:], 1)], axis=-1
    )
    return ring_place(line, after, far, before, second)


def with_squares(features, gain, gx):
    gained = features.astype(f32) * gain.astype(f32)[None, None, None, :]
    return gained.astype(bf16), squares_columns(features, gx)


def products_reduced(gained, squares, weights, y, c, cut):
    y_far, y_after, y_before = (y + 2) & 3, (y + 1) & 3, (y + 3) & 3

    def rows(array, places):
        pieces = []
        for at_y, at_c in places:
            for at_x in (2 * at_c, 2 * at_c + 1):
                at = (jnp.where(c == 0, at_y, at_x), jnp.where(c == 0, at_x, at_y), 0, 0)
                pieces.append(lax.dynamic_slice(array, at, (1, 1) + array.shape[2:])[0, 0])
        return jnp.concatenate(pieces, axis=0)

    def products(places, ahead=None):
        block = rows(gained, places)
        if ahead is not None:
            block, _ = lax.optimization_barrier((block, ahead))
        parts = [jnp.dot(block, w, preferred_element_type=f32).astype(bf16) for w in weights]
        out = jnp.concatenate(parts + [rows(squares, places)], axis=1)
        return out.reshape(len(places), 2 * gained.shape[2], -1)

    def plus(ours, theirs):
        return (ours.astype(f32) + theirs.astype(f32)).astype(bf16)

    far = products([(y_far, 1 - c), (y_far, c)])
    theirs = products([(y_after, 1 - c), (y_before, 1 - c), (y, 1 - c)], far)
    far_sum = plus(far[1], swap_core(far[0]))
    got_low = send_y(far_sum[:, :cut], 1)
    got_high = send_y(far_sum[:, cut:], -1)
    theirs_then, _ = lax.optimization_barrier((theirs, far_sum))
    swapped = swap_core(theirs_then)
    ours = products([(y_after, c), (y_before, c)], (far_sum, theirs))
    near = plus(ours, swapped[:2])
    after = jnp.concatenate([plus(near[0, :, :cut], got_low), near[0, :, cut:]], axis=1)
    before = jnp.concatenate([near[1, :, :cut], plus(near[1, :, cut:], got_high)], axis=1)
    own = products([(y, c)], (after, before))[0]
    total = own.astype(f32) + swapped[2].astype(f32)
    return total + send_y(after, 1).astype(f32) + send_y(before, -1).astype(f32)


def attend_block(query, key_new, value_new, key_cache, value_cache, lengths):
    rows_here = query.shape[0]
    cache_len = key_cache.shape[1]
    groups = key_cache.shape[2] // HEAD_DIM
    per_group = query.shape[1] // key_cache.shape[2]
    score_scale = HEAD_DIM ** (-0.5)
    grouped_q = query.reshape(rows_here, groups, per_group, HEAD_DIM)
    cached_keys = key_cache.reshape(rows_here, cache_len, groups, HEAD_DIM)
    cached_values = value_cache.reshape(rows_here, cache_len, groups, HEAD_DIM)
    scores = (
        jnp.einsum("rgqd,rlgd->rgql", grouped_q, cached_keys, preferred_element_type=f32)
        * score_scale
    )
    own_score = (
        jnp.einsum(
            "rgqd,rgd->rgq",
            grouped_q,
            key_new.reshape(rows_here, groups, HEAD_DIM),
            preferred_element_type=f32,
        )
        * score_scale
    )
    in_range = jnp.arange(cache_len)[None, :] < lengths[:, None]
    scores = jnp.where(in_range[:, None, None, :], scores, -jnp.inf)
    row_top = jnp.maximum(jnp.max(scores, axis=3), own_score)
    exp_all = jnp.exp(scores - row_top[:, :, :, None])
    exp_own = jnp.exp(own_score - row_top)
    denominator = jnp.sum(exp_all, axis=3) + exp_own
    weights_all = (exp_all / denominator[:, :, :, None]).astype(bf16)
    weight_own = (exp_own / denominator).astype(bf16)
    mixed = jnp.einsum("rgql,rlgd->rgqd", weights_all, cached_values, preferred_element_type=f32)
    own_values = value_new.astype(f32).reshape(rows_here, groups, 1, HEAD_DIM)
    mixed = mixed + weight_own.astype(f32)[:, :, :, None] * own_values
    return mixed.reshape(rows_here, per_group * groups * HEAD_DIM).astype(bf16)


def on_device(
    stream,
    attn_gain,
    ffn_gain,
    w_query,
    w_key,
    w_value,
    w_out,
    w_gate,
    w_up,
    key_cache,
    value_cache,
    lengths,
):
    rows_dev = key_cache.shape[0]
    size_gy = lax.axis_size("gy")
    rows_j = stream.shape[0]
    rows_i = 2 * rows_j
    gx, gy = lax.axis_index("gx"), lax.axis_index("gy")
    y, c = gx >> 1, gx & 1
    z, x = gy >> 2, gy & 3
    query_cols = w_query.shape[1]
    key_cols = w_key.shape[1]

    first, second = jnp.where(c == 0, x, z), jnp.where(c == 0, z, x)
    features = plane_gather(stream, first, second)
    w_kv = jnp.concatenate([w_key, w_value], axis=1)
    col_count = query_cols + 2 * key_cols
    summed = products_reduced(
        *with_squares(features, attn_gain, gx), [w_query, w_kv], y, c, query_cols // 2 + LANES
    )
    summed = (summed[:, :col_count] * row_inverse(summed[:, col_count:])).astype(bf16)

    combined = lax.all_to_all(summed, "gy", split_axis=0, concat_axis=1, tiled=True)
    blocks = combined.reshape(rows_dev, size_gy, col_count)
    query = blocks[:, :, :query_cols].reshape(rows_dev, size_gy * query_cols)
    key_new = blocks[:, :, query_cols : query_cols + key_cols].reshape(rows_dev, size_gy * key_cols)
    value_new = blocks[:, :, query_cols + key_cols :].reshape(rows_dev, size_gy * key_cols)
    heads = attend_block(query, key_new, value_new, key_cache, value_cache, lengths)
    heads_moved = lax.all_to_all(heads, "gy", split_axis=1, concat_axis=0, tiled=True)

    after = send_y(heads_moved, -1)
    before = send_y(heads_moved, 1)
    far = send_y(before, 1)
    line = ring_place(heads_moved, after, far, before, y)
    head_rows = jnp.zeros((N_Y, N_C, rows_i, heads_moved.shape[1]), bf16)
    head_rows = lax.dynamic_update_slice(head_rows, line[:, None], (0, c, 0, 0))
    head_rows = lax.dynamic_update_slice(head_rows, swap_core(line)[:, None], (0, 1 - c, 0, 0))
    head_rows = head_rows.reshape(N_Z, N_X, rows_j, -1)

    def out_part(k):
        at = (first + k) & 3
        pieces = []
        for other in range(4):
            start = (jnp.where(c == 0, other, at), jnp.where(c == 0, at, other), 0, 0)
            pieces.append(lax.dynamic_slice(head_rows, start, (1, 1, rows_j, query_cols))[0, 0])
        block = jnp.concatenate(pieces, axis=0)
        product = jnp.dot(block, w_out, preferred_element_type=f32).astype(bf16)
        return product.reshape(4, rows_j, -1)

    partial = ring_reduce(out_part(2), out_part(1), out_part(3), out_part(0), send_first)
    partial = partial.astype(bf16)

    def at_second(k):
        return lax.dynamic_index_in_dim(partial, (second + k) & 3, 0, keepdims=False)

    attn_share = ring_reduce(at_second(2), at_second(1), at_second(3), at_second(0), send_second)
    residual = (stream.astype(f32) + attn_share).astype(bf16)

    features_two = plane_gather(residual, first, second)
    split_at = w_gate.shape[1]
    gate_up = products_reduced(
        *with_squares(features_two, ffn_gain, gx), [w_gate, w_up], y, c, split_at
    )
    inverse_two = row_inverse(gate_up[:, 2 * split_at :])
    gate = gate_up[:, :split_at] * inverse_two
    up = gate_up[:, split_at : 2 * split_at] * inverse_two
    hidden = (jax.nn.silu(gate) * up).astype(bf16)
    return (residual, hidden)


def solution(mesh):
    placed = (
        P("gy", "gx"),
        P("gx"),
        P("gx"),
        P("gx", "gy"),
        P("gx", "gy"),
        P("gx", "gy"),
        P("gy", "gx"),
        P("gx", "gy"),
        P("gx", "gy"),
        P(("gx", "gy"), None, None),
        P(("gx", "gy"), None, None),
        P(("gx", "gy")),
    )
    return jax.shard_map(
        on_device,
        mesh=mesh,
        in_specs=placed,
        out_specs=(P("gy", "gx"), P("gx", "gy")),
        check_vma=False,
    )
```

```python
import jax
import jax.numpy as jnp
from jax import lax
from jax.sharding import PartitionSpec as P

D = 16384
HEAD_DIM = 128
N_Y, N_C, N_Z, N_X = 4, 2, 4, 4
LANES = 128

epsilon = 1e-05

bf16 = jnp.bfloat16
f32 = jnp.float32


def send_pairs(values, target):
    pairs = []
    for y in range(N_Y):
        for c in range(N_C):
            for z in range(N_Z):
                for x in range(N_X):
                    to_y, to_c, to_z, to_x = target(y, c, z, x)
                    source = ((y * N_C + c) * N_Z + z) * N_X + x
                    pairs.append((source, ((to_y * N_C + to_c) * N_Z + to_z) * N_X + to_x))
    return lax.ppermute(values, ("gx", "gy"), pairs)


def send_first(values, k):
    return send_pairs(values, lambda y, c, z, x: (y, c, z ^ (k * c), x ^ (k * (1 - c))))


def send_second(values, k):
    return send_pairs(values, lambda y, c, z, x: (y, c, z ^ (k * (1 - c)), x ^ (k * c)))


def send_y(values, k):
    return send_pairs(values, lambda y, c, z, x: (y ^ k, c, z, x))


def swap_core(values):
    return send_pairs(values, lambda y, c, z, x: (y, 1 - c, z, x))


def ring_place(block, one, two, three, here):
    out = jnp.zeros((4,) + block.shape, block.dtype)
    for k, piece in ((0, block), (1, one), (3, three), (2, two)):
        start = (here ^ k,) + (0,) * block.ndim
        out = lax.dynamic_update_slice(out, piece[None], start)
    return out


def plus(ours, theirs):
    return (ours.astype(f32) + theirs.astype(f32)).astype(bf16)


def ring_gather(block, send):
    one, three = send(block, 1), send(block, 3)
    cut = block.shape[-1] // 2
    low, high = send(one[..., :cut], 3), send(three[..., cut:], 1)
    return one, jnp.concatenate([low, high], axis=-1), three


def ring_reduce(own, one, two, three, send, cut):
    got_low = send(two[..., :cut], 1)
    got_high = send(two[..., cut:], 3)
    three = jnp.concatenate([plus(three[..., :cut], got_low), three[..., cut:]], axis=-1)
    got_three = send(three, 3)
    one = jnp.concatenate([one[..., :cut], plus(one[..., cut:], got_high)], axis=-1)
    got_one = send(one, 1)
    return own.astype(f32) + got_three.astype(f32) + got_one.astype(f32)


def squares_columns(values, gx):
    values_f = values.astype(f32)
    total = jnp.sum(values_f * values_f, axis=-1)
    high = lax.reduce_precision(total, 8, 7)
    rest = total - high
    middle = lax.reduce_precision(rest, 8, 7)
    low = rest - middle
    lane = lax.broadcasted_iota(jnp.int32, total.shape + (LANES,), total.ndim)
    columns = jnp.where(lane == gx, high[..., None], 0.0)
    columns = jnp.where(lane == gx + 8, middle[..., None], columns)
    columns = jnp.where(lane == gx + 16, low[..., None], columns)
    return columns.astype(bf16)


def row_inverse(columns):
    return lax.rsqrt(jnp.sum(columns, axis=1, keepdims=True) / D + epsilon)


def plane_gather(block, sends, places):
    far, one, three = sends[0](block, 2), sends[0](block, 1), sends[0](block, 3)
    line = ring_place(block, one, far, three, places[0])
    return ring_place(line, *ring_gather(line, sends[1]), places[1])


def with_squares(features, gain, gx):
    gained = features.astype(f32) * gain.astype(f32)[None, None, None, :]
    return gained.astype(bf16), squares_columns(features, gx)


def products_reduced(gained, squares, weights, z_major, y, c, cut):
    def rows(array, places):
        pieces = []
        for at_y, at_c in places:
            for at_x in (2 * at_c, 2 * at_c + 1):
                at = (jnp.where(z_major, at_y, at_x), jnp.where(z_major, at_x, at_y), 0, 0)
                pieces.append(lax.dynamic_slice(array, at, (1, 1) + array.shape[2:])[0, 0])
        return jnp.concatenate(pieces, axis=0)

    def products(places, ahead=None):
        block = rows(gained, places)
        if ahead is not None:
            block, _ = lax.optimization_barrier((block, ahead))
        parts = [jnp.dot(block, w, preferred_element_type=f32).astype(bf16) for w in weights]
        out = jnp.concatenate(parts + [rows(squares, places)], axis=1)
        return out.reshape(len(places), 2 * gained.shape[2], -1)

    far = products([(y ^ 2, 1 - c), (y ^ 2, c)])
    theirs = products([(y ^ 1, 1 - c), (y ^ 3, 1 - c), (y, 1 - c)], far)
    far_sum = plus(far[1], swap_core(far[0]))
    theirs_then, _ = lax.optimization_barrier((theirs, far_sum))
    swapped = swap_core(theirs_then)
    ours = products([(y ^ 1, c), (y ^ 3, c)], (far_sum, theirs))
    near = plus(ours, swapped[:2])
    own = products([(y, c)], near)[0]
    total = own.astype(f32) + swapped[2].astype(f32)
    return ring_reduce(total, near[0], far_sum, near[1], send_y, cut)


def attend_block(query, key_new, value_new, key_cache, value_cache, lengths):
    rows_here = query.shape[0]
    cache_len = key_cache.shape[1]
    groups = key_cache.shape[2] // HEAD_DIM
    per_group = query.shape[1] // key_cache.shape[2]
    score_scale = HEAD_DIM ** (-0.5)
    grouped_q = query.reshape(rows_here, groups, per_group, HEAD_DIM)
    cached_keys = key_cache.reshape(rows_here, cache_len, groups, HEAD_DIM)
    cached_values = value_cache.reshape(rows_here, cache_len, groups, HEAD_DIM)
    scores = (
        jnp.einsum("rgqd,rlgd->rgql", grouped_q, cached_keys, preferred_element_type=f32)
        * score_scale
    )
    own_score = (
        jnp.einsum(
            "rgqd,rgd->rgq",
            grouped_q,
            key_new.reshape(rows_here, groups, HEAD_DIM),
            preferred_element_type=f32,
        )
        * score_scale
    )
    in_range = jnp.arange(cache_len)[None, :] < lengths[:, None]
    scores = jnp.where(in_range[:, None, None, :], scores, -jnp.inf)
    row_top = jnp.maximum(jnp.max(scores, axis=3), own_score)
    exp_all = jnp.exp(scores - row_top[:, :, :, None])
    exp_own = jnp.exp(own_score - row_top)
    denominator = jnp.sum(exp_all, axis=3) + exp_own
    weights_all = (exp_all / denominator[:, :, :, None]).astype(bf16)
    weight_own = (exp_own / denominator).astype(bf16)
    mixed = jnp.einsum("rgql,rlgd->rgqd", weights_all, cached_values, preferred_element_type=f32)
    own_values = value_new.astype(f32).reshape(rows_here, groups, 1, HEAD_DIM)
    mixed = mixed + weight_own.astype(f32)[:, :, :, None] * own_values
    return mixed.reshape(rows_here, per_group * groups * HEAD_DIM).astype(bf16)


def on_device(
    stream,
    attn_gain,
    ffn_gain,
    w_query,
    w_key,
    w_value,
    w_out,
    w_gate,
    w_up,
    key_cache,
    value_cache,
    lengths,
):
    rows_dev = key_cache.shape[0]
    size_gy = lax.axis_size("gy")
    rows_j = stream.shape[0]
    rows_i = 2 * rows_j
    gx, gy = lax.axis_index("gx"), lax.axis_index("gy")
    y, c = gx >> 1, gx & 1
    z, x = gy >> 2, gy & 3
    query_cols = w_query.shape[1]
    key_cols = w_key.shape[1]

    first, second = jnp.where(c == 0, x, z), jnp.where(c == 0, z, x)
    sends, places = (send_first, send_second), (first, second)
    features = plane_gather(stream, sends, places)
    w_kv = jnp.concatenate([w_key, w_value], axis=1)
    col_count = query_cols + 2 * key_cols
    summed = products_reduced(
        *with_squares(features, attn_gain, gx), [w_query, w_kv], c == 0, y, c, query_cols // 2 + LANES
    )
    summed = (summed[:, :col_count] * row_inverse(summed[:, col_count:])).astype(bf16)

    combined = lax.all_to_all(summed, "gy", split_axis=0, concat_axis=1, tiled=True)
    blocks = combined.reshape(rows_dev, size_gy, col_count)
    query = blocks[:, :, :query_cols].reshape(rows_dev, size_gy * query_cols)
    key_new = blocks[:, :, query_cols : query_cols + key_cols].reshape(rows_dev, size_gy * key_cols)
    value_new = blocks[:, :, query_cols + key_cols :].reshape(rows_dev, size_gy * key_cols)
    heads = attend_block(query, key_new, value_new, key_cache, value_cache, lengths)
    heads_moved = lax.all_to_all(heads, "gy", split_axis=1, concat_axis=0, tiled=True)

    line = ring_place(heads_moved, *ring_gather(heads_moved, send_y), y)
    head_rows = jnp.zeros((N_Y, N_C, rows_i, heads_moved.shape[1]), bf16)
    head_rows = lax.dynamic_update_slice(head_rows, line[:, None], (0, c, 0, 0))
    head_rows = lax.dynamic_update_slice(head_rows, swap_core(line)[:, None], (0, 1 - c, 0, 0))
    head_rows = head_rows.reshape(N_Z, N_X, rows_j, -1)

    def out_part(k):
        at = first ^ k
        pieces = []
        for other in range(4):
            start = (jnp.where(c == 0, other, at), jnp.where(c == 0, at, other), 0, 0)
            pieces.append(lax.dynamic_slice(head_rows, start, (1, 1, rows_j, query_cols))[0, 0])
        block = jnp.concatenate(pieces, axis=0)
        product = jnp.dot(block, w_out, preferred_element_type=f32).astype(bf16)
        return product.reshape(4, rows_j, -1)

    partial = ring_reduce(*map(out_part, (0, 1, 2, 3)), send_first, w_out.shape[1] // 2)
    partial = partial.astype(bf16)

    def at_second(k):
        return lax.dynamic_index_in_dim(partial, second ^ k, 0, keepdims=False)

    attn_share = at_second(0).astype(f32)
    for k in (2, 1, 3):
        attn_share = attn_share + send_second(at_second(k), k).astype(f32)
    residual = (stream.astype(f32) + attn_share).astype(bf16)

    features_two = plane_gather(residual, sends, places)
    split_at = w_gate.shape[1]
    gate_up = products_reduced(
        *with_squares(features_two, ffn_gain, gx), [w_gate, w_up], c == 0, y, c, split_at
    )
    inverse_two = row_inverse(gate_up[:, 2 * split_at :])
    gate = gate_up[:, :split_at] * inverse_two
    up = gate_up[:, split_at : 2 * split_at] * inverse_two
    hidden = (jax.nn.silu(gate) * up).astype(bf16)
    return (residual, hidden)


def solution(mesh):
    placed = (
        P("gy", "gx"),
        P("gx"),
        P("gx"),
        P("gx", "gy"),
        P("gx", "gy"),
        P("gx", "gy"),
        P("gy", "gx"),
        P("gx", "gy"),
        P("gx", "gy"),
        P(("gx", "gy"), None, None),
        P(("gx", "gy"), None, None),
        P(("gx", "gy")),
    )
    return jax.shard_map(
        on_device,
        mesh=mesh,
        in_specs=placed,
        out_specs=(P("gy", "gx"), P("gx", "gy")),
        check_vma=False,
    )
```

```python
import jax
import jax.numpy as jnp
from jax import lax
from jax.sharding import PartitionSpec as P

D = 16384
HEAD_DIM = 128
N_Y, N_C, N_Z, N_X = 4, 2, 4, 4
LANES = 128

epsilon = 1e-05

bf16 = jnp.bfloat16
f32 = jnp.float32


def send_pairs(values, target):
    pairs = []
    for y in range(N_Y):
        for c in range(N_C):
            for z in range(N_Z):
                for x in range(N_X):
                    to_y, to_c, to_z, to_x = target(y, c, z, x)
                    source = ((y * N_C + c) * N_Z + z) * N_X + x
                    pairs.append((source, ((to_y * N_C + to_c) * N_Z + to_z) * N_X + to_x))
    return lax.ppermute(values, ("gx", "gy"), pairs)


def send_first(values, k):
    return send_pairs(values, lambda y, c, z, x: (y, c, z ^ (k * c), x ^ (k * (1 - c))))


def send_second(values, k):
    return send_pairs(values, lambda y, c, z, x: (y, c, z ^ (k * (1 - c)), x ^ (k * c)))


def send_y(values, k):
    return send_pairs(values, lambda y, c, z, x: (y ^ k, c, z, x))


def swap_core(values):
    return send_pairs(values, lambda y, c, z, x: (y, 1 - c, z, x))


def ring_place(block, one, two, three, here):
    out = jnp.zeros((4,) + block.shape, block.dtype)
    for k, piece in ((0, block), (1, one), (3, three), (2, two)):
        if piece is None:
            continue
        start = (here ^ k,) + (0,) * block.ndim
        out = lax.dynamic_update_slice(out, piece[None], start)
    return out


def plus(ours, theirs):
    return (ours.astype(f32) + theirs.astype(f32)).astype(bf16)


def ring_gather(block, send):
    one, three = send(block, 1), send(block, 3)
    cut = block.shape[-1] // 2
    low, high = send(one[..., :cut], 3), send(three[..., cut:], 1)
    return one, jnp.concatenate([low, high], axis=-1), three


def ring_reduce(own, one, two, three, send, cut):
    got_low = send(two[..., :cut], 1)
    got_high = send(two[..., cut:], 3)
    three = jnp.concatenate([plus(three[..., :cut], got_low), three[..., cut:]], axis=-1)
    got_three = send(three, 3)
    one = jnp.concatenate([one[..., :cut], plus(one[..., cut:], got_high)], axis=-1)
    got_one = send(one, 1)
    return own.astype(f32) + got_three.astype(f32) + got_one.astype(f32)


def squares_columns(values, gx):
    values_f = values.astype(f32)
    total = jnp.sum(values_f * values_f, axis=-1)
    high = lax.reduce_precision(total, 8, 7)
    rest = total - high
    middle = lax.reduce_precision(rest, 8, 7)
    low = rest - middle
    lane = lax.broadcasted_iota(jnp.int32, total.shape + (LANES,), total.ndim)
    columns = jnp.where(lane == gx, high[..., None], 0.0)
    columns = jnp.where(lane == gx + 8, middle[..., None], columns)
    columns = jnp.where(lane == gx + 16, low[..., None], columns)
    return columns.astype(bf16)


def row_inverse(columns):
    return lax.rsqrt(jnp.sum(columns, axis=1, keepdims=True) / D + epsilon)


def plane_gather(block, sends, places):
    far, one, three = sends[0](block, 2), sends[0](block, 1), sends[0](block, 3)
    line = ring_place(block, one, far, three, places[0])
    return ring_place(line, *ring_gather(line, sends[1]), places[1])


def with_squares(features, gain, gx):
    features, gain = lax.optimization_barrier((features, gain))
    gained = (features.astype(f32) * gain.astype(f32)).astype(bf16)
    return gained, squares_columns(features, gx)


def plane_products(block, gain, weights, sends, places, gx):
    far, one, three = sends[0](block, 2), sends[0](block, 1), sends[0](block, 3)
    line = ring_place(block, one, far, three, places[0])
    one, far, three = ring_gather(line, sends[1])
    most = ring_place(line, one, None, three, places[1])

    def products(rows):
        gained, squares = with_squares(rows, gain, gx)
        flat = gained.reshape(-1, gained.shape[-1])
        outs = [jnp.dot(flat, w, preferred_element_type=f32).astype(bf16) for w in weights]
        return [out.reshape(rows.shape[:-1] + (-1,)) for out in outs] + [squares]

    start = (places[1] ^ 2, 0, 0, 0)
    return [
        lax.dynamic_update_slice(all_rows, last[None], start)
        for all_rows, last in zip(products(most), products(far))
    ]


def reduced_rows(terms, z_major, y, c, cut):
    def rows(at_y, at_c):
        pieces = []
        for at_x in (2 * at_c, 2 * at_c + 1):
            at = (jnp.where(z_major, at_y, at_x), jnp.where(z_major, at_x, at_y), 0, 0)
            parts = [lax.dynamic_slice(t, at, (1, 1) + t.shape[2:])[0, 0] for t in terms]
            pieces.append(jnp.concatenate(parts, axis=1))
        return jnp.concatenate(pieces, axis=0)

    far = plus(rows(y ^ 2, c), swap_core(rows(y ^ 2, 1 - c)))
    theirs = jnp.stack([rows(y ^ k, 1 - c) for k in (1, 3, 0)])
    theirs, far = lax.optimization_barrier((theirs, far))
    theirs = swap_core(theirs)
    one, three = plus(rows(y ^ 1, c), theirs[0]), plus(rows(y ^ 3, c), theirs[1])
    own = rows(y, c).astype(f32) + theirs[2].astype(f32)
    return ring_reduce(own, one, far, three, send_y, cut)


def products_reduced(gained, squares, weights, z_major, y, c, cut):
    def rows(array, places):
        pieces = []
        for at_y, at_c in places:
            for at_x in (2 * at_c, 2 * at_c + 1):
                at = (jnp.where(z_major, at_y, at_x), jnp.where(z_major, at_x, at_y), 0, 0)
                pieces.append(lax.dynamic_slice(array, at, (1, 1) + array.shape[2:])[0, 0])
        return jnp.concatenate(pieces, axis=0)

    def products(places, ahead=None):
        block = rows(gained, places)
        if ahead is not None:
            block, _ = lax.optimization_barrier((block, ahead))
        parts = [jnp.dot(block, w, preferred_element_type=f32).astype(bf16) for w in weights]
        out = jnp.concatenate(parts + [rows(squares, places)], axis=1)
        return out.reshape(len(places), 2 * gained.shape[2], -1)

    far = products([(y ^ 2, 1 - c), (y ^ 2, c)])
    theirs = products([(y ^ 1, 1 - c), (y ^ 3, 1 - c), (y, 1 - c)], far)
    far_sum = plus(far[1], swap_core(far[0]))
    theirs_then, _ = lax.optimization_barrier((theirs, far_sum))
    swapped = swap_core(theirs_then)
    ours = products([(y ^ 1, c), (y ^ 3, c)], (far_sum, theirs))
    near = plus(ours, swapped[:2])
    own = products([(y, c)], near)[0]
    total = own.astype(f32) + swapped[2].astype(f32)
    return ring_reduce(total, near[0], far_sum, near[1], send_y, cut)


def attend_block(query, key_new, value_new, key_cache, value_cache, lengths):
    rows_here = query.shape[0]
    cache_len = key_cache.shape[1]
    groups = key_cache.shape[2] // HEAD_DIM
    per_group = query.shape[1] // key_cache.shape[2]
    score_scale = HEAD_DIM ** (-0.5)
    grouped_q = query.reshape(rows_here, groups, per_group, HEAD_DIM)
    cached_keys = key_cache.reshape(rows_here, cache_len, groups, HEAD_DIM)
    cached_values = value_cache.reshape(rows_here, cache_len, groups, HEAD_DIM)
    scores = (
        jnp.einsum("rgqd,rlgd->rgql", grouped_q, cached_keys, preferred_element_type=f32)
        * score_scale
    )
    own_score = (
        jnp.einsum(
            "rgqd,rgd->rgq",
            grouped_q,
            key_new.reshape(rows_here, groups, HEAD_DIM),
            preferred_element_type=f32,
        )
        * score_scale
    )
    in_range = jnp.arange(cache_len)[None, :] < lengths[:, None]
    scores = jnp.where(in_range[:, None, None, :], scores, -jnp.inf)
    row_top = jnp.maximum(jnp.max(scores, axis=3), own_score)
    exp_all = jnp.exp(scores - row_top[:, :, :, None])
    exp_own = jnp.exp(own_score - row_top)
    denominator = jnp.sum(exp_all, axis=3) + exp_own
    weights_all = (exp_all / denominator[:, :, :, None]).astype(bf16)
    weight_own = (exp_own / denominator).astype(bf16)
    mixed = jnp.einsum("rgql,rlgd->rgqd", weights_all, cached_values, preferred_element_type=f32)
    own_values = value_new.astype(f32).reshape(rows_here, groups, 1, HEAD_DIM)
    mixed = mixed + weight_own.astype(f32)[:, :, :, None] * own_values
    return mixed.reshape(rows_here, per_group * groups * HEAD_DIM).astype(bf16)


def on_device(
    stream,
    attn_gain,
    ffn_gain,
    w_query,
    w_key,
    w_value,
    w_out,
    w_gate,
    w_up,
    key_cache,
    value_cache,
    lengths,
):
    rows_dev = key_cache.shape[0]
    size_gy = lax.axis_size("gy")
    rows_j = stream.shape[0]
    rows_i = 2 * rows_j
    gx, gy = lax.axis_index("gx"), lax.axis_index("gy")
    y, c = gx >> 1, gx & 1
    z, x = gy >> 2, gy & 3
    query_cols = w_query.shape[1]
    key_cols = w_key.shape[1]

    first, second = jnp.where(c == 0, x, z), jnp.where(c == 0, z, x)
    sends, places = (send_first, send_second), (first, second)
    w_kv = jnp.concatenate([w_key, w_value], axis=1)
    col_count = query_cols + 2 * key_cols
    terms = plane_products(stream, attn_gain, [w_query, w_kv], sends, places, gx)
    summed = reduced_rows(terms, c == 0, y, c, query_cols // 2 + LANES)
    summed = (summed[:, :col_count] * row_inverse(summed[:, col_count:])).astype(bf16)

    combined = lax.all_to_all(summed, "gy", split_axis=0, concat_axis=1, tiled=True)
    blocks = combined.reshape(rows_dev, size_gy, col_count)
    query = blocks[:, :, :query_cols].reshape(rows_dev, size_gy * query_cols)
    key_new = blocks[:, :, query_cols : query_cols + key_cols].reshape(rows_dev, size_gy * key_cols)
    value_new = blocks[:, :, query_cols + key_cols :].reshape(rows_dev, size_gy * key_cols)
    heads = attend_block(query, key_new, value_new, key_cache, value_cache, lengths)
    heads_moved = lax.all_to_all(heads, "gy", split_axis=1, concat_axis=0, tiled=True)

    moved = [send_y(heads_moved, k) for k in (2, 1, 3)]
    line = ring_place(heads_moved, moved[1], moved[0], moved[2], y)
    head_rows = jnp.zeros((N_Y, N_C, rows_i, heads_moved.shape[1]), bf16)
    head_rows = lax.dynamic_update_slice(head_rows, line[:, None], (0, c, 0, 0))
    head_rows = lax.dynamic_update_slice(head_rows, swap_core(line)[:, None], (0, 1 - c, 0, 0))
    head_rows = head_rows.reshape(N_Z, N_X, rows_j, -1)

    def out_part(k):
        at = first ^ k
        pieces = []
        for other in range(4):
            start = (jnp.where(c == 0, other, at), jnp.where(c == 0, at, other), 0, 0)
            pieces.append(lax.dynamic_slice(head_rows, start, (1, 1, rows_j, query_cols))[0, 0])
        block = jnp.concatenate(pieces, axis=0)
        product = jnp.dot(block, w_out, preferred_element_type=f32).astype(bf16)
        return product.reshape(4, rows_j, -1)

    partial = ring_reduce(*map(out_part, (0, 1, 2, 3)), send_first, w_out.shape[1] // 2)
    partial = partial.astype(bf16)

    def at_second(k):
        return lax.dynamic_index_in_dim(partial, second ^ k, 0, keepdims=False)

    attn_share = at_second(0).astype(f32)
    for k in (2, 1, 3):
        attn_share = attn_share + send_second(at_second(k), k).astype(f32)
    residual = (stream.astype(f32) + attn_share).astype(bf16)

    features_two = plane_gather(residual, sends, places)
    split_at = w_gate.shape[1]
    gate_up = products_reduced(
        *with_squares(features_two, ffn_gain, gx), [w_gate, w_up], c == 0, y, c, split_at
    )
    inverse_two = row_inverse(gate_up[:, 2 * split_at :])
    gate = gate_up[:, :split_at] * inverse_two
    up = gate_up[:, split_at : 2 * split_at] * inverse_two
    hidden = (jax.nn.silu(gate) * up).astype(bf16)
    return (residual, hidden)


def solution(mesh):
    placed = (
        P("gy", "gx"),
        P("gx"),
        P("gx"),
        P("gx", "gy"),
        P("gx", "gy"),
        P("gx", "gy"),
        P("gy", "gx"),
        P("gx", "gy"),
        P("gx", "gy"),
        P(("gx", "gy"), None, None),
        P(("gx", "gy"), None, None),
        P(("gx", "gy")),
    )
    return jax.shard_map(
        on_device,
        mesh=mesh,
        in_specs=placed,
        out_specs=(P("gy", "gx"), P("gx", "gy")),
        check_vma=False,
    )
```

```python
import jax
import jax.numpy as jnp
from jax import lax
from jax.sharding import PartitionSpec as P

D = 16384
HEAD_DIM = 128
N_Y, N_C, N_Z, N_X = 4, 2, 4, 4
LANES = 128

epsilon = 1e-05

bf16 = jnp.bfloat16
f32 = jnp.float32


def send_pairs(values, target):
    pairs = []
    for y in range(N_Y):
        for c in range(N_C):
            for z in range(N_Z):
                for x in range(N_X):
                    to_y, to_c, to_z, to_x = target(y, c, z, x)
                    source = ((y * N_C + c) * N_Z + z) * N_X + x
                    pairs.append((source, ((to_y * N_C + to_c) * N_Z + to_z) * N_X + to_x))
    return lax.ppermute(values, ("gx", "gy"), pairs)


def send_first(values, k):
    return send_pairs(values, lambda y, c, z, x: (y, c, z ^ (k * c), x ^ (k * (1 - c))))


def send_second(values, k):
    return send_pairs(values, lambda y, c, z, x: (y, c, z ^ (k * (1 - c)), x ^ (k * c)))


def send_y(values, k):
    return send_pairs(values, lambda y, c, z, x: (y ^ k, c, z, x))


def swap_core(values):
    return send_pairs(values, lambda y, c, z, x: (y, 1 - c, z, x))


def ring_place(block, one, two, three, here):
    out = jnp.zeros((4,) + block.shape, block.dtype)
    for k, piece in ((0, block), (1, one), (3, three), (2, two)):
        if piece is None:
            continue
        start = (here ^ k,) + (0,) * block.ndim
        out = lax.dynamic_update_slice(out, piece[None], start)
    return out


def plus(ours, theirs):
    return (ours.astype(f32) + theirs.astype(f32)).astype(bf16)


def ring_gather(block, send):
    one, three = send(block, 1), send(block, 3)
    cut = block.shape[-1] // 2
    low, high = send(one[..., :cut], 3), send(three[..., cut:], 1)
    return one, jnp.concatenate([low, high], axis=-1), three


def ring_reduce(own, one, two, three, send, cut):
    got_low = send(two[..., :cut], 1)
    got_high = send(two[..., cut:], 3)
    three = jnp.concatenate([plus(three[..., :cut], got_low), three[..., cut:]], axis=-1)
    got_three = send(three, 3)
    one = jnp.concatenate([one[..., :cut], plus(one[..., cut:], got_high)], axis=-1)
    got_one = send(one, 1)
    return own.astype(f32) + got_three.astype(f32) + got_one.astype(f32)


def squares_columns(values, gx):
    values_f = values.astype(f32)
    total = jnp.sum(values_f * values_f, axis=-1)
    high = lax.reduce_precision(total, 8, 7)
    rest = total - high
    middle = lax.reduce_precision(rest, 8, 7)
    low = rest - middle
    lane = lax.broadcasted_iota(jnp.int32, total.shape + (LANES,), total.ndim)
    columns = jnp.where(lane == gx, high[..., None], 0.0)
    columns = jnp.where(lane == gx + 8, middle[..., None], columns)
    columns = jnp.where(lane == gx + 16, low[..., None], columns)
    return columns.astype(bf16)


def row_inverse(columns):
    return lax.rsqrt(jnp.sum(columns, axis=1, keepdims=True) / D + epsilon)


def plane_gather(block, sends, places):
    far, one, three = sends[0](block, 2), sends[0](block, 1), sends[0](block, 3)
    line = ring_place(block, one, far, three, places[0])
    return ring_place(line, *ring_gather(line, sends[1]), places[1])


def with_squares(features, gain, gx):
    features, gain = lax.optimization_barrier((features, gain))
    gained = (features.astype(f32) * gain.astype(f32)).astype(bf16)
    return gained, squares_columns(features, gx)


def plane_products(block, gain, weights, sends, places, gx):
    far, one, three = sends[0](block, 2), sends[0](block, 1), sends[0](block, 3)
    line = ring_place(block, one, far, three, places[0])
    one, far, three = ring_gather(line, sends[1])
    most = ring_place(line, one, None, three, places[1])

    def products(rows):
        gained, squares = with_squares(rows, gain, gx)
        flat = gained.reshape(-1, gained.shape[-1])
        outs = [jnp.dot(flat, w, preferred_element_type=f32).astype(bf16) for w in weights]
        return [out.reshape(rows.shape[:-1] + (-1,)) for out in outs] + [squares]

    start = (places[1] ^ 2, 0, 0, 0)
    return [
        lax.dynamic_update_slice(all_rows, last[None], start)
        for all_rows, last in zip(products(most), products(far))
    ]


def reduced_rows(terms, z_major, y, c, cut):
    def rows(at_y, at_c):
        pieces = []
        for at_x in (2 * at_c, 2 * at_c + 1):
            at = (jnp.where(z_major, at_y, at_x), jnp.where(z_major, at_x, at_y), 0, 0)
            parts = [lax.dynamic_slice(t, at, (1, 1) + t.shape[2:])[0, 0] for t in terms]
            pieces.append(jnp.concatenate(parts, axis=1))
        return jnp.concatenate(pieces, axis=0)

    far = plus(rows(y ^ 2, c), swap_core(rows(y ^ 2, 1 - c)))
    theirs = jnp.stack([rows(y ^ k, 1 - c) for k in (1, 3, 0)])
    theirs, far = lax.optimization_barrier((theirs, far))
    theirs = swap_core(theirs)
    one, three = plus(rows(y ^ 1, c), theirs[0]), plus(rows(y ^ 3, c), theirs[1])
    own = rows(y, c).astype(f32) + theirs[2].astype(f32)
    return ring_reduce(own, one, far, three, send_y, cut)


def products_reduced(gained, squares, weights, z_major, y, c, cut):
    def rows(array, places):
        pieces = []
        for at_y, at_c in places:
            for at_x in (2 * at_c, 2 * at_c + 1):
                at = (jnp.where(z_major, at_y, at_x), jnp.where(z_major, at_x, at_y), 0, 0)
                pieces.append(lax.dynamic_slice(array, at, (1, 1) + array.shape[2:])[0, 0])
        return jnp.concatenate(pieces, axis=0)

    def products(places, ahead=None):
        block = rows(gained, places)
        if ahead is not None:
            block, _ = lax.optimization_barrier((block, ahead))
        parts = [jnp.dot(block, w, preferred_element_type=f32).astype(bf16) for w in weights]
        out = jnp.concatenate(parts + [rows(squares, places)], axis=1)
        return out.reshape(len(places), 2 * gained.shape[2], -1)

    far = products([(y ^ 2, 1 - c), (y ^ 2, c)])
    theirs = products([(y ^ 1, 1 - c), (y ^ 3, 1 - c), (y, 1 - c)], far)
    far_sum = plus(far[1], swap_core(far[0]))
    theirs_then, _ = lax.optimization_barrier((theirs, far_sum))
    swapped = swap_core(theirs_then)
    ours = products([(y ^ 1, c), (y ^ 3, c)], (far_sum, theirs))
    near = plus(ours, swapped[:2])
    own = products([(y, c)], near)[0]
    total = own.astype(f32) + swapped[2].astype(f32)
    return ring_reduce(total, near[0], far_sum, near[1], send_y, cut)


def attend_block(query, key_new, value_new, key_cache, value_cache, lengths):
    rows_here = query.shape[0]
    cache_len = key_cache.shape[1]
    groups = key_cache.shape[2] // HEAD_DIM
    per_group = query.shape[1] // key_cache.shape[2]
    score_scale = HEAD_DIM ** (-0.5)
    grouped_q = query.reshape(rows_here, groups, per_group, HEAD_DIM)
    cached_keys = key_cache.reshape(rows_here, cache_len, groups, HEAD_DIM)
    cached_values = value_cache.reshape(rows_here, cache_len, groups, HEAD_DIM)
    scores = (
        jnp.einsum("rgqd,rlgd->rgql", grouped_q, cached_keys, preferred_element_type=f32)
        * score_scale
    )
    own_score = (
        jnp.einsum(
            "rgqd,rgd->rgq",
            grouped_q,
            key_new.reshape(rows_here, groups, HEAD_DIM),
            preferred_element_type=f32,
        )
        * score_scale
    )
    in_range = jnp.arange(cache_len)[None, :] < lengths[:, None]
    scores = jnp.where(in_range[:, None, None, :], scores, -jnp.inf)
    row_top = jnp.maximum(jnp.max(scores, axis=3), own_score)
    exp_all = jnp.exp(scores - row_top[:, :, :, None])
    exp_own = jnp.exp(own_score - row_top)
    denominator = jnp.sum(exp_all, axis=3) + exp_own
    weights_all = (exp_all / denominator[:, :, :, None]).astype(bf16)
    weight_own = (exp_own / denominator).astype(bf16)
    mixed = jnp.einsum("rgql,rlgd->rgqd", weights_all, cached_values, preferred_element_type=f32)
    own_values = value_new.astype(f32).reshape(rows_here, groups, 1, HEAD_DIM)
    mixed = mixed + weight_own.astype(f32)[:, :, :, None] * own_values
    return mixed.reshape(rows_here, per_group * groups * HEAD_DIM).astype(bf16)


def on_device(
    stream,
    attn_gain,
    ffn_gain,
    w_query,
    w_key,
    w_value,
    w_out,
    w_gate,
    w_up,
    key_cache,
    value_cache,
    lengths,
):
    rows_dev = key_cache.shape[0]
    size_gy = lax.axis_size("gy")
    rows_j = stream.shape[0]
    rows_i = 2 * rows_j
    gx, gy = lax.axis_index("gx"), lax.axis_index("gy")
    y, c = gx >> 1, gx & 1
    z, x = gy >> 2, gy & 3
    query_cols = w_query.shape[1]
    key_cols = w_key.shape[1]

    first, second = jnp.where(c == 0, x, z), jnp.where(c == 0, z, x)
    sends, places = (send_first, send_second), (first, second)
    w_kv = jnp.concatenate([w_key, w_value], axis=1)
    col_count = query_cols + 2 * key_cols
    terms = plane_products(stream, attn_gain, [w_query, w_kv], sends, places, gx)
    summed = reduced_rows(terms, c == 0, y, c, query_cols // 2 + LANES)
    summed = (summed[:, :col_count] * row_inverse(summed[:, col_count:])).astype(bf16)

    combined = lax.all_to_all(summed, "gy", split_axis=0, concat_axis=1, tiled=True)
    blocks = combined.reshape(rows_dev, size_gy, col_count)
    query = blocks[:, :, :query_cols].reshape(rows_dev, size_gy * query_cols)
    key_new = blocks[:, :, query_cols : query_cols + key_cols].reshape(rows_dev, size_gy * key_cols)
    value_new = blocks[:, :, query_cols + key_cols :].reshape(rows_dev, size_gy * key_cols)
    heads = attend_block(query, key_new, value_new, key_cache, value_cache, lengths)
    heads_moved = lax.all_to_all(heads, "gy", split_axis=1, concat_axis=0, tiled=True)

    moved = [send_y(heads_moved, k) for k in (2, 1, 3)]
    line = ring_place(heads_moved, moved[1], moved[0], moved[2], y)
    head_rows = jnp.zeros((N_Y, N_C, rows_i, heads_moved.shape[1]), bf16)
    head_rows = lax.dynamic_update_slice(head_rows, line[:, None], (0, c, 0, 0))
    head_rows = lax.dynamic_update_slice(head_rows, swap_core(line)[:, None], (0, 1 - c, 0, 0))
    head_rows = head_rows.reshape(N_Z, N_X, rows_j, -1)

    def out_part(k):
        at = first ^ k
        pieces = []
        for other in range(4):
            start = (jnp.where(c == 0, other, at), jnp.where(c == 0, at, other), 0, 0)
            pieces.append(lax.dynamic_slice(head_rows, start, (1, 1, rows_j, query_cols))[0, 0])
        block = jnp.concatenate(pieces, axis=0)
        product = jnp.dot(block, w_out, preferred_element_type=f32).astype(bf16)
        return product.reshape(4, rows_j, -1)

    partial = ring_reduce(*map(out_part, (0, 1, 2, 3)), send_first, w_out.shape[1] // 2)
    partial = partial.astype(bf16)

    def at_second(k):
        return lax.dynamic_index_in_dim(partial, second ^ k, 0, keepdims=False)

    attn_share = at_second(0).astype(f32)
    for k in (2, 1, 3):
        attn_share = attn_share + send_second(at_second(k), k).astype(f32)
    residual = (stream.astype(f32) + attn_share).astype(bf16)

    features_two = plane_gather(residual, sends[::-1], places[::-1])
    split_at = w_gate.shape[1]
    gate_up = products_reduced(
        *with_squares(features_two, ffn_gain, gx), [w_gate, w_up], c == 1, y, c, split_at
    )
    inverse_two = row_inverse(gate_up[:, 2 * split_at :])
    gate = gate_up[:, :split_at] * inverse_two
    up = gate_up[:, split_at : 2 * split_at] * inverse_two
    hidden = (jax.nn.silu(gate) * up).astype(bf16)
    return (residual, hidden)


def solution(mesh):
    placed = (
        P("gy", "gx"),
        P("gx"),
        P("gx"),
        P("gx", "gy"),
        P("gx", "gy"),
        P("gx", "gy"),
        P("gy", "gx"),
        P("gx", "gy"),
        P("gx", "gy"),
        P(("gx", "gy"), None, None),
        P(("gx", "gy"), None, None),
        P(("gx", "gy")),
    )
    return jax.shard_map(
        on_device,
        mesh=mesh,
        in_specs=placed,
        out_specs=(P("gy", "gx"), P("gx", "gy")),
        check_vma=False,
    )
```
